32 devices in a mesh: gx: 4 (over y, x), gy: 2 (over core), gz: 4 (over z).
Axes of the slice: x: 2, y: 2, z: 4, core: 2. Of those that a mesh axis runs over, the one named last changes fastest.
Arguments:
- positions: float32 [3, 16, 8, 8, 128], P(None, 'gx', 'gy', 'gz'), may hold values from 0 to 128, as said below
- grain_radii: float32 [16, 8, 8, 128], P('gx', 'gy', 'gz'), may hold values from 0.4 to 0.6
- film_liquid: float32 [16, 8, 8, 128], P('gx', 'gy', 'gz'), may hold values from 0.5 to 2
- pair_live: int32 [4, 2, 4, 864], P('gx', 'gy', 'gz'), may hold values from 0 to 1, as said below
- partner: int32 [4, 2, 4, 864, 128], P('gx', 'gy', 'gz'), may hold values from 0 to 127, as said below
- rupture: int32 [4, 2, 4, 864, 128], P('gx', 'gy', 'gz'), may hold values from 0 to 1
- volume: float32 [4, 2, 4, 864, 128], P('gx', 'gy', 'gz'), may hold values from 0.005 to 0.05
Outputs:
- forces: float32 [3, 16, 8, 8, 128], P(None, 'gx', 'gy', 'gz')
- film_next: float32 [16, 8, 8, 128], P('gx', 'gy', 'gz')
- volume_next: float32 [4, 2, 4, 864, 128], P('gx', 'gy', 'gz')
The draws below stay inside these ranges and needn't reach their ends.
Inputs may be any that keep to these rules, and one draw needn't show every extreme that they name: `pair_live`: slot s of a device is 1 only if its tile pair lies inside the grid; every pair of distinct touching tiles is listed at most once over all devices, by one of its two tiles; the slot of a tile with itself (s % 27 = 13) is always 1. partner[s, m] is never m itself. `positions`: the grains of tile (p, q, r) lie in its box, 8 wide along the first dimension and 4 along the others, the boxes side by side from the root; no two grains are closer than 0.5.
All inputs are finite; a program needn't handle non-finite values.
Results may differ from the reference program's by a relative error of at most 0.0003.
Values sent between devices are 32-bit elements; how exact they have to be, the bound alone decides.
A program may use at most 64 MiB of HBM per device.

```python
import math
import jax
import jax.numpy as jnp
from jax import lax

GRAINS = 128
BX = 4
BY = 4
BZ = 2
SLOTS = 864
TX = 16
TY = 8
TZ = 8
N_GX = 4
N_GY = 2
N_GZ = 4


shell_offsets = [(along_x, along_y, along_z) for along_x in (-1, 0, 1) for along_y in (-1, 0, 1) for along_z in (-1, 0, 1)]


def site_tables(key):
    scores = jax.random.randint(jax.random.fold_in(key, 41), (TX, TY, TZ, GRAINS), 0, 1048576)
    distinct = scores * GRAINS + jnp.arange(GRAINS, dtype=jnp.int32)
    site_of = jnp.argsort(distinct, axis=-1).astype(jnp.int32)
    grain_at = jnp.argsort(site_of, axis=-1).astype(jnp.int32)
    return (site_of, grain_at)


def draw_positions(key, part):
    site_of = site_tables(key)[0]
    spread = GRAINS // 16
    jitter = jax.random.uniform(key, (3, TX, TY, TZ, GRAINS), jnp.float32, -0.25, 0.25)
    root_x = (jnp.arange(TX, dtype=jnp.int32) * spread).astype(jnp.float32)[:, None, None, None]
    root_y = (jnp.arange(TY, dtype=jnp.int32) * 4).astype(jnp.float32)[None, :, None, None]
    root_z = (jnp.arange(TZ, dtype=jnp.int32) * 4).astype(jnp.float32)[None, None, :, None]
    coord_x = root_x + (site_of // 16).astype(jnp.float32) + 0.5 + jitter[0]
    coord_y = root_y + (site_of // 4 % 4).astype(jnp.float32) + 0.5 + jitter[1]
    coord_z = root_z + (site_of % 4).astype(jnp.float32) + 0.5 + jitter[2]
    return jnp.stack([coord_x, coord_y, coord_z], axis=0)


def bridge_links(key):
    subkeys = jax.random.split(jax.random.fold_in(key, 29), 3)
    site_of, grain_at = site_tables(key)
    layers = GRAINS // 16
    slot_total = 27 * BX * BY * BZ
    shape = (N_GX, N_GY, N_GZ, slot_total, GRAINS)
    full = (N_GX, N_GY, N_GZ, slot_total)
    slot = jnp.arange(slot_total, dtype=jnp.int32)
    tile = slot // 27
    code = slot % 27
    step_x = code // 9 - 1
    step_y = code // 3 % 3 - 1
    step_z = code % 3 - 1
    anchor_x = jnp.broadcast_to((jnp.arange(N_GX, dtype=jnp.int32) * BX)[:, None, None, None] + (tile // (BY * BZ))[None, None, None, :], full)
    anchor_y = jnp.broadcast_to((jnp.arange(N_GY, dtype=jnp.int32) * BY)[None, :, None, None] + (tile // BZ % BY)[None, None, None, :], full)
    anchor_z = jnp.broadcast_to((jnp.arange(N_GZ, dtype=jnp.int32) * BZ)[None, None, :, None] + (tile % BZ)[None, None, None, :], full)
    other_x = jnp.clip(anchor_x + step_x, 0, TX - 1)
    other_y = jnp.clip(anchor_y + step_y, 0, TY - 1)
    other_z = jnp.clip(anchor_z + step_z, 0, TZ - 1)
    site = site_of[anchor_x, anchor_y, anchor_z]
    site_x = site // 16
    site_y = site // 4 % 4
    site_z = site % 4
    heading = jax.random.randint(subkeys[0], shape, 0, 6)
    along = heading // 2
    sign = 2 * (heading % 2) - 1
    target_x = site_x + sign * (along == 0).astype(jnp.int32) - step_x[:, None] * layers
    target_y = site_y + sign * (along == 1).astype(jnp.int32) - step_y[:, None] * 4
    target_z = site_z + sign * (along == 2).astype(jnp.int32) - step_z[:, None] * 4
    inside = (target_x >= 0) & (target_x < layers) & (target_y >= 0) & (target_y < 4) & (target_z >= 0) & (target_z < 4)
    target_site = jnp.where(inside, target_x * 16 + target_y * 4 + target_z, 0).astype(jnp.int32)
    neighbour = jnp.take_along_axis(grain_at[other_x, other_y, other_z], target_site, axis=-1)
    grain = jnp.arange(GRAINS, dtype=jnp.int32)
    stride = jax.random.randint(subkeys[1], shape, 1, GRAINS)
    fallback = (grain + stride) % GRAINS
    partner = jnp.where(inside, neighbour, fallback).astype(jnp.int32)
    chance = jax.random.randint(subkeys[2], shape, 0, 4)
    rupture = jnp.where(inside, (chance == 0).astype(jnp.int32), (chance < 2).astype(jnp.int32)).astype(jnp.int32)
    return (partner, rupture)


def draw_partner(key, part):
    return bridge_links(key)[0]


def draw_rupture(key, part):
    return bridge_links(key)[1]


def draw_pair_live(key, part):
    subkeys = jax.random.split(jax.random.fold_in(key, 11), 3)
    level = jax.random.randint(subkeys[0], (N_GX, N_GY, N_GZ), 1, 7)
    level = jnp.repeat(jnp.repeat(jnp.repeat(level, BX, axis=0), BY, axis=1), BZ, axis=2)
    chance = jax.random.randint(subkeys[1], (13, TX, TY, TZ), 0, 12)
    owner = jax.random.randint(subkeys[2], (13, TX, TY, TZ), 0, 2)
    padded_level = jnp.pad(level, 1)
    inside = jnp.pad(jnp.ones((TX, TY, TZ), jnp.int32), 1)
    table = [jnp.zeros((TX, TY, TZ), jnp.int32) for number in range(27)]
    table[13] = jnp.ones((TX, TY, TZ), jnp.int32)
    upper_half = [offset for offset in shell_offsets if offset > (0, 0, 0)]
    for number, offset in enumerate(upper_half):
        start = (1 + offset[0], 1 + offset[1], 1 + offset[2])
        limit = (1 + offset[0] + TX, 1 + offset[1] + TY, 1 + offset[2] + TZ)
        near_level = lax.slice(padded_level, start, limit)
        near_inside = lax.slice(inside, start, limit)
        listed = (chance[number] < level + near_level) & (near_inside == 1)
        here = (listed & (owner[number] == 0)).astype(jnp.int32)
        there = (listed & (owner[number] == 1)).astype(jnp.int32)
        back_start = (1 - offset[0], 1 - offset[1], 1 - offset[2])
        back_limit = (1 - offset[0] + TX, 1 - offset[1] + TY, 1 - offset[2] + TZ)
        moved = lax.slice(jnp.pad(there, 1), back_start, back_limit)
        table[shell_offsets.index(offset)] = here
        table[shell_offsets.index((-offset[0], -offset[1], -offset[2]))] = moved
    stacked = jnp.stack(table, axis=-1)
    shaped = stacked.reshape(N_GX, BX, N_GY, BY, N_GZ, BZ, 27).transpose(0, 2, 4, 1, 3, 5, 6)
    return shaped.reshape(N_GX, N_GY, N_GZ, 27 * BX * BY * BZ)


def block_scale(stream_key, extent, shards, smallest, largest):
    level = 1.0
    for position, blocks in shards:
        steps = jax.random.uniform(jax.random.fold_in(jax.random.fold_in(stream_key, 6), position), (blocks,), jnp.float32, smallest / len(shards), largest / len(shards))
        level = level * jnp.repeat(jnp.exp(steps), extent[position] // blocks).reshape((-1,) + (1,) * (len(extent) - 1 - position))
    return level


def setup_inputs(seed: int = 0) -> dict:
    key_of = jax.random.split(jax.random.key(seed), 8)
    return {
        "positions": draw_positions(jax.random.fold_in(key_of[7], 71), 0),
        "grain_radii": jnp.clip(0.4 + 0.20000002 * jax.random.uniform(key_of[1], (TX, TY, TZ, GRAINS), jnp.float32) ** block_scale(key_of[1], (TX, TY, TZ, GRAINS), ((0, 4), (1, 2), (2, 4)), -0.2, 0.2), 0.4, 0.6),
        "film_liquid": jnp.clip(0.5 + 1.5 * jax.random.uniform(key_of[2], (TX, TY, TZ, GRAINS), jnp.float32) ** block_scale(key_of[2], (TX, TY, TZ, GRAINS), ((0, 4), (1, 2), (2, 4)), -0.2, 0.2), 0.5, 2.0),
        "pair_live": draw_pair_live(jax.random.fold_in(key_of[7], 71), 0),
        "partner": draw_partner(jax.random.fold_in(key_of[7], 71), 0),
        "rupture": draw_rupture(jax.random.fold_in(key_of[7], 71), 0),
        "volume": jnp.clip(jnp.exp(math.log(0.05) - 2.3025851 * jax.random.uniform(key_of[6], (N_GX, N_GY, N_GZ, SLOTS, GRAINS), jnp.float32) ** block_scale(key_of[6], (N_GX, N_GY, N_GZ, SLOTS, GRAINS), ((0, 4), (1, 2), (2, 4)), -0.2, 0.2)), 0.005, 0.05),
    }


ABSORB = 0.02
shell_offsets = [(along_x, along_y, along_z) for along_x in (-1, 0, 1) for along_y in (-1, 0, 1) for along_z in (-1, 0, 1)]

def evaluate(pieces):
    anchor, others, centre, active, partner, rupture, volume = pieces
    grains = anchor.shape[-1]
    identity = jnp.eye(grains, dtype=jnp.float32)
    diagonal = identity[None] * centre[:, None, None]
    deltas = [anchor[:, component, :, None] - others[:, component, None, :] for component in range(3)]
    squares = deltas[0] * deltas[0] + deltas[1] * deltas[1] + deltas[2] * deltas[2] + diagonal
    distance = jnp.sqrt(squares)
    reach_sum = anchor[:, 3, :, None] + others[:, 3, None, :]
    reduced = anchor[:, 3, :, None] * others[:, 3, None, :] / reach_sum
    intersection = jnp.maximum(reach_sum - distance, 0.0) * (1.0 - diagonal)
    repulse = jnp.sqrt(reduced) * intersection * jnp.sqrt(intersection) / distance * active[:, None, None]
    products = [repulse * member for member in deltas]
    keep_other = (1.0 - centre)[:, None]
    contact_a = jnp.stack([lax.optimization_barrier(jnp.sum(member, axis=2)) for member in products], axis=1)
    contact_b = jnp.stack([-lax.optimization_barrier(jnp.sum(member, axis=1)) * keep_other for member in products], axis=1)
    choose = (partner[:, :, None] == jnp.arange(grains, dtype=jnp.int32)[None, None, :]).astype(jnp.float32)
    matched = jnp.einsum('ncj,nij->nci', others, choose, precision=lax.Precision.HIGHEST)
    gap_vec = anchor[:, :3] - matched[:, :3]
    spacing = jnp.sqrt(lax.optimization_barrier(jnp.sum(gap_vec * gap_vec, axis=1)))
    radius_sum = anchor[:, 3] + matched[:, 3]
    harmonic = 2.0 * anchor[:, 3] * matched[:, 3] / radius_sum
    scaled_gap = jnp.maximum(spacing - radius_sum, 0.0) * jnp.sqrt(harmonic / volume)
    broken = rupture.astype(jnp.float32)
    intact = active[:, None] * (1.0 - broken)
    tension = intact * harmonic / (1.0 + 1.05 * scaled_gap + 2.5 * scaled_gap * scaled_gap) / spacing
    bridge_force = tension[:, None, :] * gap_vec
    released = active[:, None] * broken * volume
    volume_next = intact * (volume + ABSORB * (anchor[:, 4] + matched[:, 4]))
    liquid_anchor = 0.5 * released - ABSORB * intact * anchor[:, 4]
    liquid_other = 0.5 * released - ABSORB * intact * matched[:, 4]
    reaction = jnp.einsum('nci,nij->ncj', jnp.concatenate([bridge_force, liquid_other[:, None]], axis=1), choose, precision=lax.Precision.HIGHEST)
    anchor_side = jnp.concatenate([contact_a - bridge_force, liquid_anchor[:, None]], axis=1)
    other_side = jnp.concatenate([contact_b, jnp.zeros_like(liquid_anchor)[:, None]], axis=1) + reaction
    return (anchor_side, other_side, volume_next)

def tile_order(values):
    extra = values.shape[4:]
    shaped = values.reshape((N_GX, N_GY, N_GZ, BX, BY, BZ, 27) + extra)
    permute = (0, 3, 1, 4, 2, 5, 6) + tuple(range(7, 7 + len(extra)))
    return shaped.transpose(permute).reshape((TX, TY, TZ, 27) + extra)

def reference(positions, grain_radii, film_liquid, pair_live, partner, rupture, volume):
    grain_state = jnp.concatenate([positions, grain_radii[None], film_liquid[None]], axis=0)
    padded = jnp.pad(grain_state, ((0, 0), (1, 1), (1, 1), (1, 1), (0, 0)))
    tile_count = TX * TY * TZ
    groups = tile_count // (BX * BY * BZ)
    active = tile_order(pair_live).astype(jnp.float32)
    partners = tile_order(partner)
    ruptures = tile_order(rupture)
    volumes = tile_order(volume)
    anchor = grain_state.reshape(5, tile_count, GRAINS).transpose(1, 0, 2)
    totals = jnp.zeros((4, TX + 2, TY + 2, TZ + 2, GRAINS), jnp.float32)
    updated = []
    for number, offset in enumerate(shell_offsets):
        start = (0, 1 + offset[0], 1 + offset[1], 1 + offset[2], 0)
        limit = (5, 1 + offset[0] + TX, 1 + offset[1] + TY, 1 + offset[2] + TZ, GRAINS)
        others = lax.slice(padded, start, limit).reshape(5, tile_count, GRAINS).transpose(1, 0, 2)
        centre = jnp.full((tile_count,), 1.0 if number == 13 else 0.0, jnp.float32)
        pieces = (anchor, others, centre, active[:, :, :, number].reshape(tile_count), partners[:, :, :, number].reshape(tile_count, GRAINS), ruptures[:, :, :, number].reshape(tile_count, GRAINS), volumes[:, :, :, number].reshape(tile_count, GRAINS))
        blocked = jax.tree.map(lambda member: member.reshape((groups, tile_count // groups) + member.shape[1:]), pieces)
        anchor_side, other_side, fresh = lax.map(evaluate, blocked)
        anchor_side = anchor_side.reshape(tile_count, 4, GRAINS).transpose(1, 0, 2).reshape(4, TX, TY, TZ, GRAINS)
        other_side = other_side.reshape(tile_count, 4, GRAINS).transpose(1, 0, 2).reshape(4, TX, TY, TZ, GRAINS)
        totals = totals.at[:, 1:TX + 1, 1:TY + 1, 1:TZ + 1].add(anchor_side)
        totals = totals.at[:, 1 + offset[0]:1 + offset[0] + TX, 1 + offset[1]:1 + offset[1] + TY, 1 + offset[2]:1 + offset[2] + TZ].add(other_side)
        updated.append(fresh.reshape(TX, TY, TZ, GRAINS))
    stacked = jnp.stack(updated, axis=3).reshape(N_GX, BX, N_GY, BY, N_GZ, BZ, 27, GRAINS)
    volume_next = stacked.transpose(0, 2, 4, 1, 3, 5, 6, 7).reshape(N_GX, N_GY, N_GZ, 27 * BX * BY * BZ, GRAINS)
    interior = totals[:, 1:TX + 1, 1:TY + 1, 1:TZ + 1]
    return (interior[:3], film_liquid + interior[3], volume_next)
```

```python
import functools

import jax
import jax.numpy as jnp
from jax import lax
from jax.experimental import pallas as pl
from jax.experimental.pallas import tpu as pltpu
from jax.sharding import PartitionSpec as P

ABSORB = 0.02
TINY = 1e-30
FLOOR = 1e-12


def padded(cells, sides, width):
    for axis, dim in sides:
        count = lax.axis_size(axis)
        ends = count - 1
        head = lax.slice_in_dim(cells, 0, width, axis=dim)
        tail = lax.slice_in_dim(cells, cells.shape[dim] - width, cells.shape[dim], axis=dim)
        cells = jnp.concatenate(
            [
                lax.ppermute(tail, axis, [(i, (i + 1) % count) for i in range(ends)]),
                cells,
                lax.ppermute(head, axis, [((i + 1) % count, i) for i in range(ends)]),
            ],
            axis=dim,
        )
    return cells


def fold(totals, sides):
    for axis, dim in sides:
        count = lax.axis_size(axis)
        ends = count - 1
        size = totals.shape[dim]
        low = lax.slice_in_dim(totals, 0, 1, axis=dim)
        high = lax.slice_in_dim(totals, size - 1, size, axis=dim)
        inner = lax.slice_in_dim(totals, 1, size - 1, axis=dim)
        from_left = lax.ppermute(high, axis, [(i, (i + 1) % count) for i in range(ends)])
        from_right = lax.ppermute(low, axis, [((i + 1) % count, i) for i in range(ends)])
        length = size - 2
        widths = [(0, 0)] * totals.ndim
        widths[dim] = (0, length - 1)
        other = [(0, 0)] * totals.ndim
        other[dim] = (length - 1, 0)
        totals = inner + jnp.pad(from_left, widths) + jnp.pad(from_right, other)
    return totals


def split(values):
    high = values.astype(jnp.bfloat16)
    low = (values - high.astype(jnp.float32)).astype(jnp.bfloat16)
    return high, low


def kernel(
    dims,
    live_smem,
    border_ref,
    flags_ref,
    partner_ref,
    rupture_ref,
    volume_ref,
    totals_ref,
    fresh_ref,
    rows,
    table,
    others,
    held,
    acc,
    far,
    near,
    listed,
):
    bx, by, bz, grains = dims
    wy, wz = by + 2, bz + 2
    blocks = grains // 8
    plane = by * bz
    step = pl.program_id(0)
    cells = (bx + 2) * wy * wz

    @pl.when(step == 0)
    def _():
        far[...] = jnp.zeros_like(far)
        near[...] = jnp.zeros_like(near)
        held[...] = jnp.zeros_like(held)
        others[...] = jnp.full_like(others, 1.0)
        for ix in range(bx + 2):
            for iy in range(wy):
                base = (ix * wy + iy) * wz
                for c in range(5):
                    rows[c, base : base + wz, :] = border_ref[c, ix, iy]
                rows[5, base : base + wz, :] = 1.0 / jnp.maximum(border_ref[3, ix, iy], 0.1)

    def tile_step(local, carry):
        iy = local // bz
        iz = local % bz
        cell = ((step + 1) * wy + iy + 1) * wz + iz + 1
        first = local * 27
        count = jnp.int32(0)
        for s in range(27):
            listed[count] = s
            count = count + live_smem[(step * plane + local) * 27 + s]
        own = [rows[c, pl.ds(cell, 1), :] for c in range(6)]
        pad_rows = jnp.zeros((2, grains), jnp.float32)
        columns = jnp.concatenate([own[0], own[1], own[2], own[3], own[5], own[4], pad_rows], 0).T
        for c in range(5):
            table[c] = jnp.broadcast_to(columns[:, c : c + 1], (grains, grains))
        for ex in range(3):
            for ey in range(3):
                start = cell + ((ex - 1) * wy + (ey - 1)) * wz - 1
                at = ex * 9 + ey * 3
                for c in range(5):
                    others[c, at : at + 3, :] = rows[c, pl.ds(start, 3), :]
        partner = partner_ref[pl.ds(first, 27), :]
        got = [jnp.take_along_axis(others[c, 0:27, :], partner, axis=1) for c in range(5)]
        gap = [own[c] - got[c] for c in range(3)]
        spacing = jnp.sqrt(gap[0] * gap[0] + gap[1] * gap[1] + gap[2] * gap[2])
        radius_sum = own[3] + got[3]
        harmonic = 2.0 * own[3] * got[3] / radius_sum
        vol = volume_ref[pl.ds(first, 27), :]
        scaled = jnp.maximum(spacing - radius_sum, 0.0) * jnp.sqrt(harmonic / vol)
        active = flags_ref[pl.ds(first, 27), :]
        broken = rupture_ref[pl.ds(first, 27), :].astype(jnp.float32)
        intact = active * (1.0 - broken)
        tension = jnp.where(
            intact > 0.0, harmonic / (1.0 + 1.05 * scaled + 2.5 * scaled * scaled) / spacing, 0.0
        )
        force = [tension * member for member in gap]
        released = 0.5 * active * broken * vol
        fresh_ref[pl.ds(first, 27), :] = intact * (vol + ABSORB * (own[4] + got[4]))
        liquid_a = released - ABSORB * intact * own[4]
        liquid_b = released - ABSORB * intact * got[4]
        for c, member in enumerate(force + [liquid_b]):
            held[pl.ds(c, 27, stride=8), :] = member
        anchor_sums = [-jnp.sum(member, axis=0, keepdims=True) for member in force]
        anchor_sums.append(jnp.sum(liquid_a, axis=0, keepdims=True))
        acc[...] = jnp.zeros_like(acc)
        lanes = lax.broadcasted_iota(jnp.int32, (grains, grains), 0)

        def slot_step(k, carry):
            s = listed[k]
            target = cell + (s // 9 - 1) * (wy * wz) + (s // 3 % 3 - 1) * wz + (s % 3 - 1)
            values = held[pl.ds(pl.multiple_of(s * 8, 8), 8), :]
            high, low = split(values)
            chosen = (lanes == partner_ref[pl.ds(first + s, 1), :]).astype(jnp.float32)
            moved = lax.dot_general(
                jnp.concatenate([high, low], 0),
                chosen.astype(jnp.bfloat16),
                (((1,), (1,)), ((), ())),
                preferred_element_type=jnp.float32,
            )
            near[target] += moved[0:8] + moved[8:16]
            x, y, z, r, q = [
                jnp.broadcast_to(rows[c, pl.ds(target, 1), :], (8, grains)) for c in (0, 1, 2, 3, 5)
            ]
            sums = [jnp.zeros((8, grains), jnp.float32)] * 3
            for m in range(blocks):
                part = slice(8 * m, 8 * m + 8)
                dx = table[0, part] - x
                dy = table[1, part] - y
                dz = table[2, part] - z
                square = jnp.maximum(dx * dx + dy * dy + dz * dz, FLOOR)
                inverse = lax.rsqrt(square)
                inter = jnp.maximum(table[3, part] + r - square * inverse, TINY)
                push = inter * inter * inverse * lax.rsqrt(inter * (table[4, part] + q))
                for c, member in enumerate((dx, dy, dz)):
                    product = push * member
                    acc[c, part] += product
                    sums[c] = sums[c] + product
            keep = jnp.where(s == 13, 0.0, 1.0)
            for c in range(3):
                far[target, c] += sums[c] * keep
            return carry

        lax.fori_loop(0, count, slot_step, 0)
        ones = jnp.ones((8, grains), jnp.bfloat16)
        row = lax.broadcasted_iota(jnp.int32, (8, grains), 0)
        added = jnp.zeros((8, grains), jnp.float32)
        for c in range(4):
            value = anchor_sums[c]
            if c < 3:
                high, low = split(acc[c])
                dims_t = (((1,), (1,)), ((), ()))
                value = value + lax.dot_general(
                    ones, high, dims_t, preferred_element_type=jnp.float32
                )
                value = value + lax.dot_general(
                    ones, low, dims_t, preferred_element_type=jnp.float32
                )
            added = added + jnp.where(row == c, value, 0.0)
        near[cell] += added
        return carry

    lax.fori_loop(0, plane, tile_step, 0)

    @pl.when(step == pl.num_programs(0) - 1)
    def _():
        row = lax.broadcasted_iota(jnp.int32, (8, grains), 0)

        def finish(cell, carry):
            value = near[cell]
            for c in range(3):
                total = jnp.sum(far[cell, c], axis=0, keepdims=True)
                value = value - jnp.where(row == c, total, 0.0)
            totals_ref[cell] = value
            return carry

        lax.fori_loop(0, cells, finish, 0)


def shards(positions, grain_radii, film_liquid, pair_live, partner, rupture, volume):
    bx, by, bz, grains = grain_radii.shape
    tiles = bx * by * bz
    slots = 27 * tiles
    cells = (bx + 2) * (by + 2) * (bz + 2)
    state = jnp.concatenate([positions, grain_radii[None], film_liquid[None]], axis=0)
    sides = (("gx", 1), ("gy", 2), ("gz", 3))
    border = padded(state, sides, 1)
    live = pair_live.reshape(slots)
    flags = jnp.broadcast_to(live.astype(jnp.float32)[:, None], (slots, grains))
    span = 27 * by * bz
    wide = pl.BlockSpec((span, grains), lambda i, _: (i, 0))
    height = -(-cells // 8) * 8
    totals, fresh = pl.pallas_call(
        functools.partial(kernel, (bx, by, bz, grains)),
        grid_spec=pltpu.PrefetchScalarGridSpec(
            num_scalar_prefetch=1,
            grid=(bx,),
            in_specs=[
                pl.BlockSpec(border.shape, lambda i, _: (0, 0, 0, 0, 0)),
                wide,
                wide,
                wide,
                wide,
            ],
            out_specs=[pl.BlockSpec((cells, 8, grains), lambda i, _: (0, 0, 0)), wide],
            scratch_shapes=[
                pltpu.VMEM((6, height, grains), jnp.float32),
                pltpu.VMEM((5, grains, grains), jnp.float32),
                pltpu.VMEM((5, 32, grains), jnp.float32),
                pltpu.VMEM((8 * 32, grains), jnp.float32),
                pltpu.VMEM((3, grains, grains), jnp.float32),
                pltpu.VMEM((cells, 3, 8, grains), jnp.float32),
                pltpu.VMEM((cells, 8, grains), jnp.float32),
                pltpu.SMEM((32,), jnp.int32),
            ],
        ),
        out_shape=[
            jax.ShapeDtypeStruct((cells, 8, grains), jnp.float32),
            jax.ShapeDtypeStruct((slots, grains), jnp.float32),
        ],
        name="slots",
    )(
        live,
        border,
        flags,
        partner.reshape(slots, grains),
        rupture.reshape(slots, grains),
        volume.reshape(slots, grains),
    )
    totals = totals.reshape(bx + 2, by + 2, bz + 2, 8, grains)[:, :, :, :4]
    folded = fold(totals, (("gz", 2), ("gy", 1), ("gx", 0))).transpose(3, 0, 1, 2, 4)
    return (folded[:3], film_liquid + folded[3], fresh.reshape(1, 1, 1, slots, grains))


def solution(mesh):
    return jax.shard_map(
        shards,
        mesh=mesh,
        in_specs=(
            P(None, "gx", "gy", "gz", None),
            P("gx", "gy", "gz", None),
            P("gx", "gy", "gz", None),
            P("gx", "gy", "gz", None),
            P("gx", "gy", "gz", None, None),
            P("gx", "gy", "gz", None, None),
            P("gx", "gy", "gz", None, None),
        ),
        out_specs=(
            P(None, "gx", "gy", "gz", None),
            P("gx", "gy", "gz", None),
            P("gx", "gy", "gz", None, None),
        ),
        check_vma=False,
    )
```

```python
import functools

import jax
import jax.numpy as jnp
from jax import lax
from jax.experimental import pallas as pl
from jax.experimental.pallas import tpu as pltpu
from jax.sharding import PartitionSpec as P

ABSORB = 0.02
TINY = 1e-30
FLOOR = 1e-12


def neighbours():
    return [
        (ex, ey, ez)
        for ex in (-1, 0, 1)
        for ey in (-1, 0, 1)
        for ez in (-1, 0, 1)
        if (ex, ey, ez) != (0, 0, 0)
    ]


AXES = ("gx", "gy", "gz")


def present(offset):
    found = None
    for axis, shift in zip(AXES, offset):
        if shift == 0:
            continue
        place = lax.axis_index(axis) + shift
        here = (place >= 0) & (place < lax.axis_size(axis))
        found = here if found is None else found & here
    return found


def device_at(offset):
    return tuple(lax.axis_index(axis) + shift for axis, shift in zip(AXES, offset))


def opposite(offset):
    return tuple(-shift for shift in offset)


def greet(offsets):
    barrier = pltpu.get_barrier_semaphore()
    count = jnp.int32(0)
    for offset in offsets:
        here = present(offset)
        count = count + here.astype(jnp.int32)

        @pl.when(here)
        def _():
            pl.semaphore_signal(
                barrier, inc=1, device_id=device_at(offset), device_id_type=pl.DeviceIdType.MESH
            )

    pl.semaphore_wait(barrier, count)


def cut(offset, extents, low, whole, high):
    pick = []
    for shift, extent in zip(offset, extents):
        if shift < 0:
            pick.append(pl.ds(low(extent), 1))
        elif shift > 0:
            pick.append(pl.ds(high(extent), 1))
        else:
            pick.append(pl.ds(whole, extent))
    return tuple(pick)


def rim(offset, extents):
    return cut(offset, extents, lambda n: 0, 1, lambda n: n + 1)


def edge(offset, extents):
    return cut(offset, extents, lambda n: 0, 0, lambda n: n - 1)


def spread_kernel(extents, state_ref, border_ref, send_sem, recv_sem):
    offsets = neighbours()
    greet(offsets)
    copies = []
    for i, offset in enumerate(offsets):
        copy = pltpu.make_async_remote_copy(
            src_ref=state_ref.at[edge(offset, extents)],
            dst_ref=border_ref.at[rim(opposite(offset), extents)],
            send_sem=send_sem.at[i],
            recv_sem=recv_sem.at[i],
            device_id=device_at(offset),
            device_id_type=pl.DeviceIdType.MESH,
        )
        copies.append(copy)
        pl.when(present(offset))(copy.start)
    border_ref[rim((0, 0, 0), extents)] = state_ref[...]
    for offset in offsets:

        @pl.when(jnp.logical_not(present(offset)))
        def _():
            region = rim(offset, extents)
            shape = tuple(p.size for p in region) + border_ref.shape[3:]
            border_ref[region] = jnp.zeros(shape, jnp.float32)

    for offset, copy in zip(offsets, copies):
        pl.when(present(offset))(copy.wait_send)
        pl.when(present(opposite(offset)))(copy.wait_recv)


def return_kernel(extents, totals_ref, out_ref, *scratch):
    offsets = neighbours()
    inbox, (send_sem, recv_sem) = scratch[:-2], scratch[-2:]
    greet(offsets)
    copies = []
    for i, offset in enumerate(offsets):
        copy = pltpu.make_async_remote_copy(
            src_ref=totals_ref.at[rim(offset, extents)],
            dst_ref=inbox[i],
            send_sem=send_sem.at[i],
            recv_sem=recv_sem.at[i],
            device_id=device_at(offset),
            device_id_type=pl.DeviceIdType.MESH,
        )
        copies.append(copy)
        pl.when(present(offset))(copy.start)
    out_ref[...] = totals_ref[rim((0, 0, 0), extents)]
    for i, (offset, copy) in enumerate(zip(offsets, copies)):

        @pl.when(present(opposite(offset)))
        def _():
            copy.wait_recv()
            region = edge(opposite(offset), extents)
            out_ref[region] = out_ref[region] + inbox[i][...]

    for offset, copy in zip(offsets, copies):
        pl.when(present(offset))(copy.wait_send)


def spread(state, extents):
    sems = pltpu.SemaphoreType.DMA((26,))
    vmem = pl.BlockSpec(memory_space=pltpu.VMEM)
    shape = tuple(n + 2 for n in extents) + state.shape[3:]
    return pl.pallas_call(
        functools.partial(spread_kernel, extents),
        out_shape=jax.ShapeDtypeStruct(shape, jnp.float32),
        in_specs=[vmem],
        out_specs=vmem,
        scratch_shapes=[sems, sems],
        compiler_params=pltpu.CompilerParams(collective_id=0, has_side_effects=True),
        name="spread",
    )(state)


def collect(totals, extents):
    sems = pltpu.SemaphoreType.DMA((26,))
    vmem = pl.BlockSpec(memory_space=pltpu.VMEM)
    tail = totals.shape[3:]
    boxes = [
        pltpu.VMEM(tuple(1 if e else n for e, n in zip(offset, extents)) + tail, jnp.float32)
        for offset in neighbours()
    ]
    return pl.pallas_call(
        functools.partial(return_kernel, extents),
        out_shape=jax.ShapeDtypeStruct(tuple(extents) + tail, jnp.float32),
        in_specs=[vmem],
        out_specs=vmem,
        scratch_shapes=boxes + [sems, sems],
        compiler_params=pltpu.CompilerParams(collective_id=1, has_side_effects=True),
        name="collect",
    )(totals)


def split(values):
    high = values.astype(jnp.bfloat16)
    low = (values - high.astype(jnp.float32)).astype(jnp.bfloat16)
    return high, low


def kernel(
    dims,
    live_smem,
    border_ref,
    flags_ref,
    partner_ref,
    rupture_ref,
    volume_ref,
    totals_ref,
    fresh_ref,
    rows,
    table,
    others,
    held,
    acc,
    far,
    near,
    listed,
):
    bx, by, bz, grains = dims
    wy, wz = by + 2, bz + 2
    blocks = grains // 8
    plane = by * bz
    step = pl.program_id(0)
    cells = (bx + 2) * wy * wz

    @pl.when(step == 0)
    def _():
        far[...] = jnp.zeros_like(far)
        near[...] = jnp.zeros_like(near)
        held[...] = jnp.zeros_like(held)
        others[...] = jnp.full_like(others, 1.0)

        def arrange(cell, carry):
            for c in range(6):
                rows[c, pl.ds(cell, 1), :] = border_ref[cell, c : c + 1, :]
            return carry

        lax.fori_loop(0, cells, arrange, 0)

    def tile_step(local, carry):
        iy = local // bz
        iz = local % bz
        cell = ((step + 1) * wy + iy + 1) * wz + iz + 1
        first = local * 27
        count = jnp.int32(0)
        for s in range(27):
            listed[count] = s
            count = count + live_smem[(step * plane + local) * 27 + s]
        own = [rows[c, pl.ds(cell, 1), :] for c in range(6)]
        pad_rows = jnp.zeros((2, grains), jnp.float32)
        columns = jnp.concatenate([own[0], own[1], own[2], own[3], own[5], own[4], pad_rows], 0).T
        for c in range(5):
            table[c] = jnp.broadcast_to(columns[:, c : c + 1], (grains, grains))
        for ex in range(3):
            for ey in range(3):
                start = cell + ((ex - 1) * wy + (ey - 1)) * wz - 1
                at = ex * 9 + ey * 3
                for c in range(5):
                    others[c, at : at + 3, :] = rows[c, pl.ds(start, 3), :]
        partner = partner_ref[pl.ds(first, 27), :]
        got = [jnp.take_along_axis(others[c, 0:27, :], partner, axis=1) for c in range(5)]
        gap = [own[c] - got[c] for c in range(3)]
        spacing = jnp.sqrt(gap[0] * gap[0] + gap[1] * gap[1] + gap[2] * gap[2])
        radius_sum = own[3] + got[3]
        harmonic = 2.0 * own[3] * got[3] / radius_sum
        vol = volume_ref[pl.ds(first, 27), :]
        scaled = jnp.maximum(spacing - radius_sum, 0.0) * jnp.sqrt(harmonic / vol)
        active = flags_ref[pl.ds(first, 27), :]
        broken = rupture_ref[pl.ds(first, 27), :].astype(jnp.float32)
        intact = active * (1.0 - broken)
        tension = jnp.where(
            intact > 0.0, harmonic / (1.0 + 1.05 * scaled + 2.5 * scaled * scaled) / spacing, 0.0
        )
        force = [tension * member for member in gap]
        released = 0.5 * active * broken * vol
        fresh_ref[pl.ds(first, 27), :] = intact * (vol + ABSORB * (own[4] + got[4]))
        liquid_a = released - ABSORB * intact * own[4]
        liquid_b = released - ABSORB * intact * got[4]
        for c, member in enumerate(force + [liquid_b]):
            held[pl.ds(c, 27, stride=8), :] = member
        anchor_sums = [-jnp.sum(member, axis=0, keepdims=True) for member in force]
        anchor_sums.append(jnp.sum(liquid_a, axis=0, keepdims=True))
        acc[...] = jnp.zeros_like(acc)
        lanes = lax.broadcasted_iota(jnp.int32, (grains, grains), 0)

        def slot_step(k, carry):
            s = listed[k]
            target = cell + (s // 9 - 1) * (wy * wz) + (s // 3 % 3 - 1) * wz + (s % 3 - 1)
            values = held[pl.ds(pl.multiple_of(s * 8, 8), 8), :]
            high, low = split(values)
            chosen = (lanes == partner_ref[pl.ds(first + s, 1), :]).astype(jnp.float32)
            moved = lax.dot_general(
                jnp.concatenate([high, low], 0),
                chosen.astype(jnp.bfloat16),
                (((1,), (1,)), ((), ())),
                preferred_element_type=jnp.float32,
            )
            near[target] += moved[0:8] + moved[8:16]
            x, y, z, r, q = [
                jnp.broadcast_to(rows[c, pl.ds(target, 1), :], (8, grains)) for c in (0, 1, 2, 3, 5)
            ]
            sums = [jnp.zeros((8, grains), jnp.float32)] * 3
            for m in range(blocks):
                part = slice(8 * m, 8 * m + 8)
                dx = table[0, part] - x
                dy = table[1, part] - y
                dz = table[2, part] - z
                square = jnp.maximum(dx * dx + dy * dy + dz * dz, FLOOR)
                inverse = lax.rsqrt(square)
                inter = jnp.maximum(table[3, part] + r - square * inverse, TINY)
                push = inter * inter * inverse * lax.rsqrt(inter * (table[4, part] + q))
                for c, member in enumerate((dx, dy, dz)):
                    product = push * member
                    acc[c, part] += product
                    sums[c] = sums[c] + product
            keep = jnp.where(s == 13, 0.0, 1.0)
            for c in range(3):
                far[target, c] += sums[c] * keep
            return carry

        lax.fori_loop(0, count, slot_step, 0)
        ones = jnp.ones((8, grains), jnp.bfloat16)
        row = lax.broadcasted_iota(jnp.int32, (8, grains), 0)
        added = jnp.zeros((8, grains), jnp.float32)
        for c in range(4):
            value = anchor_sums[c]
            if c < 3:
                high, low = split(acc[c])
                dims_t = (((1,), (1,)), ((), ()))
                value = value + lax.dot_general(
                    ones, high, dims_t, preferred_element_type=jnp.float32
                )
                value = value + lax.dot_general(
                    ones, low, dims_t, preferred_element_type=jnp.float32
                )
            added = added + jnp.where(row == c, value, 0.0)
        near[cell] += added
        return carry

    lax.fori_loop(0, plane, tile_step, 0)

    @pl.when(step == pl.num_programs(0) - 1)
    def _():
        row = lax.broadcasted_iota(jnp.int32, (8, grains), 0)

        def finish(cell, carry):
            value = near[cell]
            for c in range(3):
                total = jnp.sum(far[cell, c], axis=0, keepdims=True)
                value = value - jnp.where(row == c, total, 0.0)
            totals_ref[cell] = value[0:4]
            return carry

        lax.fori_loop(0, cells, finish, 0)


def shards(positions, grain_radii, film_liquid, pair_live, partner, rupture, volume):
    bx, by, bz, grains = grain_radii.shape
    tiles = bx * by * bz
    slots = 27 * tiles
    cells = (bx + 2) * (by + 2) * (bz + 2)
    extents = (bx, by, bz)
    zero = jnp.zeros_like(grain_radii)
    parts = [positions[c] for c in range(3)]
    parts += [grain_radii, film_liquid, 1.0 / grain_radii, zero, zero]
    state = jnp.stack(parts, axis=3)
    border = spread(state, extents).reshape(cells, 8, grains)
    live = pair_live.reshape(slots)
    flags = jnp.broadcast_to(live.astype(jnp.float32)[:, None], (slots, grains))
    span = 27 * by * bz
    wide = pl.BlockSpec((span, grains), lambda i, _: (i, 0))
    height = -(-cells // 8) * 8
    totals, fresh = pl.pallas_call(
        functools.partial(kernel, (bx, by, bz, grains)),
        grid_spec=pltpu.PrefetchScalarGridSpec(
            num_scalar_prefetch=1,
            grid=(bx,),
            in_specs=[
                pl.BlockSpec(border.shape, lambda i, _: (0, 0, 0)),
                wide,
                wide,
                wide,
                wide,
            ],
            out_specs=[pl.BlockSpec((cells, 4, grains), lambda i, _: (0, 0, 0)), wide],
            scratch_shapes=[
                pltpu.VMEM((6, height, grains), jnp.float32),
                pltpu.VMEM((5, grains, grains), jnp.float32),
                pltpu.VMEM((5, 32, grains), jnp.float32),
                pltpu.VMEM((8 * 32, grains), jnp.float32),
                pltpu.VMEM((3, grains, grains), jnp.float32),
                pltpu.VMEM((cells, 3, 8, grains), jnp.float32),
                pltpu.VMEM((cells, 8, grains), jnp.float32),
                pltpu.SMEM((32,), jnp.int32),
            ],
        ),
        out_shape=[
            jax.ShapeDtypeStruct((cells, 4, grains), jnp.float32),
            jax.ShapeDtypeStruct((slots, grains), jnp.float32),
        ],
        name="slots",
    )(
        live,
        border,
        flags,
        partner.reshape(slots, grains),
        rupture.reshape(slots, grains),
        volume.reshape(slots, grains),
    )
    totals = totals.reshape(bx + 2, by + 2, bz + 2, 4, grains)
    folded = collect(totals, extents).transpose(3, 0, 1, 2, 4)
    return (folded[:3], film_liquid + folded[3], fresh.reshape(1, 1, 1, slots, grains))


def solution(mesh):
    return jax.shard_map(
        shards,
        mesh=mesh,
        in_specs=(
            P(None, "gx", "gy", "gz", None),
            P("gx", "gy", "gz", None),
            P("gx", "gy", "gz", None),
            P("gx", "gy", "gz", None),
            P("gx", "gy", "gz", None, None),
            P("gx", "gy", "gz", None, None),
            P("gx", "gy", "gz", None, None),
        ),
        out_specs=(
            P(None, "gx", "gy", "gz", None),
            P("gx", "gy", "gz", None),
            P("gx", "gy", "gz", None, None),
        ),
        check_vma=False,
    )
```

```python
import functools

import jax
import jax.numpy as jnp
from jax import lax
from jax.experimental import pallas as pl
from jax.experimental.pallas import tpu as pltpu
from jax.sharding import PartitionSpec as P

ABSORB = 0.02
TINY = 1e-30
RADIUS_MAX = 0.6
SLACK = 4e-3
AWAY = -1e4
FLOOR = 1e-12


def neighbours():
    return [
        (ex, ey, ez)
        for ex in (-1, 0, 1)
        for ey in (-1, 0, 1)
        for ez in (-1, 0, 1)
        if (ex, ey, ez) != (0, 0, 0)
    ]


AXES = ("gx", "gy", "gz")


def present(offset):
    found = None
    for axis, shift in zip(AXES, offset):
        if shift == 0:
            continue
        place = lax.axis_index(axis) + shift
        here = (place >= 0) & (place < lax.axis_size(axis))
        found = here if found is None else found & here
    return found


def device_at(offset):
    return tuple(lax.axis_index(axis) + shift for axis, shift in zip(AXES, offset))


def opposite(offset):
    return tuple(-shift for shift in offset)


def greet(offsets):
    barrier = pltpu.get_barrier_semaphore()
    count = jnp.int32(0)
    for offset in offsets:
        here = present(offset)
        count = count + here.astype(jnp.int32)

        @pl.when(here)
        def _():
            pl.semaphore_signal(
                barrier, inc=1, device_id=device_at(offset), device_id_type=pl.DeviceIdType.MESH
            )

    pl.semaphore_wait(barrier, count)


def cut(offset, extents, low, whole, high):
    pick = []
    for shift, extent in zip(offset, extents):
        if shift < 0:
            pick.append(pl.ds(low(extent), 1))
        elif shift > 0:
            pick.append(pl.ds(high(extent), 1))
        else:
            pick.append(pl.ds(whole, extent))
    return tuple(pick)


def rim(offset, extents):
    return cut(offset, extents, lambda n: 0, 1, lambda n: n + 1)


def edge(offset, extents):
    return cut(offset, extents, lambda n: 0, 0, lambda n: n - 1)


def spread_kernel(extents, state_ref, border_ref, send_sem, recv_sem):
    offsets = neighbours()
    greet(offsets)
    copies = []
    for i, offset in enumerate(offsets):
        copy = pltpu.make_async_remote_copy(
            src_ref=state_ref.at[edge(offset, extents)],
            dst_ref=border_ref.at[rim(opposite(offset), extents)],
            send_sem=send_sem.at[i],
            recv_sem=recv_sem.at[i],
            device_id=device_at(offset),
            device_id_type=pl.DeviceIdType.MESH,
        )
        copies.append(copy)
        pl.when(present(offset))(copy.start)
    border_ref[rim((0, 0, 0), extents)] = state_ref[...]
    for offset in offsets:

        @pl.when(jnp.logical_not(present(offset)))
        def _():
            region = rim(offset, extents)
            shape = tuple(p.size for p in region) + border_ref.shape[3:]
            border_ref[region] = jnp.zeros(shape, jnp.float32)

    for offset, copy in zip(offsets, copies):
        pl.when(present(offset))(copy.wait_send)
        pl.when(present(opposite(offset)))(copy.wait_recv)


def return_kernel(extents, totals_ref, out_ref, *scratch):
    offsets = neighbours()
    inbox, (send_sem, recv_sem) = scratch[:-2], scratch[-2:]
    greet(offsets)
    copies = []
    for i, offset in enumerate(offsets):
        copy = pltpu.make_async_remote_copy(
            src_ref=totals_ref.at[rim(offset, extents)],
            dst_ref=inbox[i],
            send_sem=send_sem.at[i],
            recv_sem=recv_sem.at[i],
            device_id=device_at(offset),
            device_id_type=pl.DeviceIdType.MESH,
        )
        copies.append(copy)
        pl.when(present(offset))(copy.start)
    out_ref[...] = totals_ref[rim((0, 0, 0), extents)]
    for i, (offset, copy) in enumerate(zip(offsets, copies)):

        @pl.when(present(opposite(offset)))
        def _():
            copy.wait_recv()
            region = edge(opposite(offset), extents)
            out_ref[region] = out_ref[region] + inbox[i][...]

    for offset, copy in zip(offsets, copies):
        pl.when(present(offset))(copy.wait_send)


def spread(state, extents):
    sems = pltpu.SemaphoreType.DMA((26,))
    vmem = pl.BlockSpec(memory_space=pltpu.VMEM)
    shape = tuple(n + 2 for n in extents) + state.shape[3:]
    return pl.pallas_call(
        functools.partial(spread_kernel, extents),
        out_shape=jax.ShapeDtypeStruct(shape, jnp.float32),
        in_specs=[vmem],
        out_specs=vmem,
        scratch_shapes=[sems, sems],
        compiler_params=pltpu.CompilerParams(collective_id=0, has_side_effects=True),
        name="spread",
    )(state)


def collect(totals, extents):
    sems = pltpu.SemaphoreType.DMA((26,))
    vmem = pl.BlockSpec(memory_space=pltpu.VMEM)
    tail = totals.shape[3:]
    boxes = [
        pltpu.VMEM(tuple(1 if e else n for e, n in zip(offset, extents)) + tail, jnp.float32)
        for offset in neighbours()
    ]
    return pl.pallas_call(
        functools.partial(return_kernel, extents),
        out_shape=jax.ShapeDtypeStruct(tuple(extents) + tail, jnp.float32),
        in_specs=[vmem],
        out_specs=vmem,
        scratch_shapes=boxes + [sems, sems],
        compiler_params=pltpu.CompilerParams(collective_id=1, has_side_effects=True),
        name="collect",
    )(totals)


def split(values):
    high = values.astype(jnp.bfloat16)
    low = (values - high.astype(jnp.float32)).astype(jnp.bfloat16)
    return high, low


def kernel(
    dims,
    live_smem,
    border_ref,
    flags_ref,
    partner_ref,
    rupture_ref,
    volume_ref,
    totals_ref,
    fresh_ref,
    rows,
    table,
    others,
    held,
    acc,
    far,
    near,
    listed,
    meets,
):
    bx, by, bz, grains = dims
    wy, wz = by + 2, bz + 2
    blocks = grains // 8
    plane = by * bz
    step = pl.program_id(0)
    cells = (bx + 2) * wy * wz

    @pl.when(step == 0)
    def _():
        far[...] = jnp.zeros_like(far)
        near[...] = jnp.zeros_like(near)
        held[...] = jnp.zeros_like(held)
        others[...] = jnp.full_like(others, 1.0)

        def arrange(cell, carry):
            for c in range(6):
                rows[c, pl.ds(cell, 1), :] = border_ref[cell, c : c + 1, :]
            return carry

        lax.fori_loop(0, cells, arrange, 0)
        for c in range(6):
            idle = AWAY if c < 3 else 0.5
            rows[c, cells : cells + 1, :] = jnp.full((1, grains), idle, jnp.float32)

    slot_of = lax.broadcasted_iota(jnp.int32, (27, grains), 0)
    up = (slot_of >= 9).astype(jnp.int32) + (slot_of >= 18).astype(jnp.int32)
    rest = slot_of - 9 * up
    over = (rest >= 3).astype(jnp.int32) + (rest >= 6).astype(jnp.int32)
    shifts = [(n - 1).astype(jnp.float32) for n in (up, over, rest - 3 * over)]
    length = jnp.sqrt(jnp.maximum(sum(e * e for e in shifts), 1.0))
    reach = 2.0 * RADIUS_MAX * length + SLACK
    weights = []
    for part in range(2):
        place = slot_of - 14 * part
        inside = (place >= 0) & (place < 14)
        power = jnp.left_shift(1, jnp.where(inside, place, 0)).astype(jnp.float32)
        weights.append(jnp.where(inside, power, 0.0))

    def tile_step(local, carry):
        iy = local // bz
        iz = local % bz
        cell = ((step + 1) * wy + iy + 1) * wz + iz + 1
        first = local * 27
        own = [rows[c, pl.ds(cell, 1), :] for c in range(6)]
        pad_rows = jnp.zeros((2, grains), jnp.float32)
        columns = jnp.concatenate([own[0], own[1], own[2], own[3], own[5], own[4], pad_rows], 0).T
        for c in range(5):
            table[c] = jnp.broadcast_to(columns[:, c : c + 1], (grains, grains))
        for ex in range(3):
            for ey in range(3):
                start = cell + ((ex - 1) * wy + (ey - 1)) * wz - 1
                at = ex * 9 + ey * 3
                for c in range(5):
                    others[c, at : at + 3, :] = rows[c, pl.ds(start, 3), :]
        partner = partner_ref[pl.ds(first, 27), :]
        ahead = sum(e * others[c, 0:27, :] for c, e in enumerate(shifts))
        behind = sum(e * own[c] for c, e in enumerate(shifts))
        apart = jnp.min(ahead, axis=1, keepdims=True) - jnp.max(behind, axis=1, keepdims=True)
        touching = apart < reach[:, 0:1]
        bits = [
            jnp.sum(jnp.where(touching, w[:, 0:1], 0.0), axis=0, keepdims=True).astype(jnp.int32)[0, 0]
            for w in weights
        ]
        count = jnp.int32(0)
        touch_count = jnp.int32(0)
        for s in range(27):
            live = live_smem[(step * plane + local) * 27 + s]
            listed[count] = s
            count = count + live
            meets[touch_count] = s
            touch_count = touch_count + live * ((bits[s // 14] >> (s % 14)) & 1)
        got = [jnp.take_along_axis(others[c, 0:27, :], partner, axis=1) for c in range(5)]
        gap = [own[c] - got[c] for c in range(3)]
        spacing = jnp.sqrt(gap[0] * gap[0] + gap[1] * gap[1] + gap[2] * gap[2])
        radius_sum = own[3] + got[3]
        harmonic = 2.0 * own[3] * got[3] / radius_sum
        vol = volume_ref[pl.ds(first, 27), :]
        scaled = jnp.maximum(spacing - radius_sum, 0.0) * jnp.sqrt(harmonic / vol)
        active = flags_ref[pl.ds(first, 27), :]
        broken = rupture_ref[pl.ds(first, 27), :].astype(jnp.float32)
        intact = active * (1.0 - broken)
        tension = jnp.where(
            intact > 0.0, harmonic / (1.0 + 1.05 * scaled + 2.5 * scaled * scaled) / spacing, 0.0
        )
        force = [tension * member for member in gap]
        released = 0.5 * active * broken * vol
        fresh_ref[pl.ds(first, 27), :] = intact * (vol + ABSORB * (own[4] + got[4]))
        liquid_a = released - ABSORB * intact * own[4]
        liquid_b = released - ABSORB * intact * got[4]
        for c, member in enumerate(force + [liquid_b]):
            held[pl.ds(c, 27, stride=8), :] = member
        anchor_sums = [-jnp.sum(member, axis=0, keepdims=True) for member in force]
        anchor_sums.append(jnp.sum(liquid_a, axis=0, keepdims=True))
        acc[...] = jnp.zeros_like(acc)
        lanes = lax.broadcasted_iota(jnp.int32, (grains, grains), 0)

        def cell_of(s):
            place = cell + (s // 9 - 1) * (wy * wz) + (s // 3 % 3 - 1) * wz + (s % 3 - 1)
            return jnp.where(s == 27, cells, place)

        def slot_step(k, carry):
            moves = []
            for n in range(3):
                at = 3 * k + n
                s = jnp.where(at < count, listed[at], 27)
                values = held[pl.ds(pl.multiple_of(s * 8, 8), 8), :]
                high, low = split(values)
                line = jnp.minimum(first + s, 27 * plane - 1)
                chosen = (lanes == partner_ref[pl.ds(line, 1), :]).astype(jnp.float32)
                moved = lax.dot_general(
                    jnp.concatenate([high, low], 0),
                    chosen.astype(jnp.bfloat16),
                    (((1,), (1,)), ((), ())),
                    preferred_element_type=jnp.float32,
                )
                moves.append((cell_of(s), moved))
            targets, keeps, fields, sums = [], [], [], []
            for n in range(2):
                at = 2 * k + n
                s = jnp.where(at < touch_count, meets[at], 27)
                target = cell_of(s)
                targets.append(target)
                keeps.append(jnp.where(s == 13, 0.0, 1.0))
                fields.append(
                    [
                        jnp.broadcast_to(rows[c, pl.ds(target, 1), :], (8, grains))
                        for c in (0, 1, 2, 3, 5)
                    ]
                )
                sums.append([jnp.zeros((8, grains), jnp.float32)] * 3)
            for m in range(blocks):
                part = slice(8 * m, 8 * m + 8)
                mine = [table[c, part] for c in range(5)]
                both = [None] * 3
                for n in range(2):
                    x, y, z, r, q = fields[n]
                    dx = mine[0] - x
                    dy = mine[1] - y
                    dz = mine[2] - z
                    square = jnp.maximum(dx * dx + dy * dy + dz * dz, FLOOR)
                    inverse = lax.rsqrt(square)
                    inter = jnp.maximum(mine[3] + r - square * inverse, TINY)
                    push = inter * inter * inverse * lax.rsqrt(inter * (mine[4] + q))
                    for c, member in enumerate((dx, dy, dz)):
                        product = push * member
                        both[c] = product if both[c] is None else both[c] + product
                        sums[n][c] = sums[n][c] + product
                for c in range(3):
                    acc[c, part] += both[c]
            for n in range(2):
                for c in range(3):
                    far[targets[n], c] += sums[n][c] * keeps[n]
            for target, moved in moves:
                near[target] += moved[0:8] + moved[8:16]
            return carry

        passes = jnp.maximum((touch_count + 1) // 2, (count + 2) // 3)
        lax.fori_loop(0, passes, slot_step, 0)
        ones = jnp.ones((8, grains), jnp.bfloat16)
        row = lax.broadcasted_iota(jnp.int32, (8, grains), 0)
        added = jnp.zeros((8, grains), jnp.float32)
        for c in range(4):
            value = anchor_sums[c]
            if c < 3:
                high, low = split(acc[c])
                dims_t = (((1,), (1,)), ((), ()))
                value = value + lax.dot_general(
                    ones, high, dims_t, preferred_element_type=jnp.float32
                )
                value = value + lax.dot_general(
                    ones, low, dims_t, preferred_element_type=jnp.float32
                )
            added = added + jnp.where(row == c, value, 0.0)
        near[cell] += added
        return carry

    lax.fori_loop(0, plane, tile_step, 0)

    @pl.when(step == pl.num_programs(0) - 1)
    def _():
        row = lax.broadcasted_iota(jnp.int32, (8, grains), 0)

        def finish(cell, carry):
            value = near[cell]
            for c in range(3):
                total = jnp.sum(far[cell, c], axis=0, keepdims=True)
                value = value - jnp.where(row == c, total, 0.0)
            totals_ref[cell] = value[0:4]
            return carry

        lax.fori_loop(0, cells, finish, 0)


def shards(positions, grain_radii, film_liquid, pair_live, partner, rupture, volume):
    bx, by, bz, grains = grain_radii.shape
    tiles = bx * by * bz
    slots = 27 * tiles
    cells = (bx + 2) * (by + 2) * (bz + 2)
    extents = (bx, by, bz)
    zero = jnp.zeros_like(grain_radii)
    parts = [positions[c] for c in range(3)]
    parts += [grain_radii, film_liquid, 1.0 / grain_radii, zero, zero]
    state = jnp.stack(parts, axis=3)
    border = spread(state, extents).reshape(cells, 8, grains)
    live = pair_live.reshape(slots)
    flags = jnp.broadcast_to(live.astype(jnp.float32)[:, None], (slots, grains))
    span = 27 * by * bz
    wide = pl.BlockSpec((span, grains), lambda i, _: (i, 0))
    height = cells // 8 * 8 + 8
    totals, fresh = pl.pallas_call(
        functools.partial(kernel, (bx, by, bz, grains)),
        grid_spec=pltpu.PrefetchScalarGridSpec(
            num_scalar_prefetch=1,
            grid=(bx,),
            in_specs=[
                pl.BlockSpec(border.shape, lambda i, _: (0, 0, 0)),
                wide,
                wide,
                wide,
                wide,
            ],
            out_specs=[pl.BlockSpec((cells, 4, grains), lambda i, _: (0, 0, 0)), wide],
            scratch_shapes=[
                pltpu.VMEM((6, height, grains), jnp.float32),
                pltpu.VMEM((5, grains, grains), jnp.float32),
                pltpu.VMEM((5, 32, grains), jnp.float32),
                pltpu.VMEM((8 * 32, grains), jnp.float32),
                pltpu.VMEM((3, grains, grains), jnp.float32),
                pltpu.VMEM((cells + 1, 3, 8, grains), jnp.float32),
                pltpu.VMEM((cells + 1, 8, grains), jnp.float32),
                pltpu.SMEM((48,), jnp.int32),
                pltpu.SMEM((32,), jnp.int32),
            ],
        ),
        out_shape=[
            jax.ShapeDtypeStruct((cells, 4, grains), jnp.float32),
            jax.ShapeDtypeStruct((slots, grains), jnp.float32),
        ],
        name="slots",
    )(
        live,
        border,
        flags,
        partner.reshape(slots, grains),
        rupture.reshape(slots, grains),
        volume.reshape(slots, grains),
    )
    totals = totals.reshape(bx + 2, by + 2, bz + 2, 4, grains)
    folded = collect(totals, extents).transpose(3, 0, 1, 2, 4)
    return (folded[:3], film_liquid + folded[3], fresh.reshape(1, 1, 1, slots, grains))


def solution(mesh):
    return jax.shard_map(
        shards,
        mesh=mesh,
        in_specs=(
            P(None, "gx", "gy", "gz", None),
            P("gx", "gy", "gz", None),
            P("gx", "gy", "gz", None),
            P("gx", "gy", "gz", None),
            P("gx", "gy", "gz", None, None),
            P("gx", "gy", "gz", None, None),
            P("gx", "gy", "gz", None, None),
        ),
        out_specs=(
            P(None, "gx", "gy", "gz", None),
            P("gx", "gy", "gz", None),
            P("gx", "gy", "gz", None, None),
        ),
        check_vma=False,
    )
```
